32 devices in a mesh: row: 4 (over y, x), col: 4 (over z), head: 2 (over core).
Axes of the slice: x: 2, y: 2, z: 4, core: 2. Of those that a mesh axis runs over, the one named last changes fastest.
Arguments:
- tokens: bfloat16 [64, 256, 384], P('row', 'col'), may hold values from -9 to 9
- tissue: int32 [64, 256], P('row', 'col'), may hold values 0 or 1
- global_pos: int32 [256], replicated, may hold values from 0 to 16383, as said below
- w_query: bfloat16 [384, 384], P(None, 'head'), may hold values from -1.5 to 1.5
- w_keyval: bfloat16 [384, 2, 384], P(None, None, 'head'), may hold values from -1.5 to 1.5
- w_out: bfloat16 [384, 384], P('head'), may hold values from -0.3125 to 0.3125
Outputs:
- mixed: bfloat16 [64, 256, 384], P('row', 'col', 'head')
The draws below stay inside these ranges and needn't reach their ends.
Inputs may be any that keep to these rules, and one draw needn't show every extreme that they name: `global_pos`: 256 distinct flat positions image row * 256 + image column.
All inputs are finite; a program needn't handle non-finite values. No bound on the sum of `tissue` on one device may be relied on, other than what follows from the above.
Results may differ from the reference program's by a relative error of at most 0.00175.
The reference program's roundings to bfloat16 on the way (of `normed`, `query` and `attn`) count: a program that leaves them out, or rounds other values in their place, can miss the bound.
Values may be sent and summed in bfloat16 or wider, within the bound.
No kernel may reach another device: no remote copies, remote signals or barrier semaphores. Data moves between devices by JAX's collectives and lax.ppermute only.
A program may use at most 128 MiB of HBM per device.

```python
import math
import jax
import jax.numpy as jnp
from jax import lax

D = 384
HEADS = 6
HEAD_DIM = 64
GLOBALS = 256
WIN = 7
BR = 8
BC = 16
CH = 16
CW = 64
H = 64
W = 256
N_ROW = 4
N_COL = 4


outlier_gain = 50.0


def global_positions(key):
    shuffled = jax.random.permutation(jax.random.fold_in(key, 11), H * W)
    return shuffled[:GLOBALS].astype(jnp.int32)


def shared_pattern(key):
    shuffled = jax.random.permutation(jax.random.fold_in(key, 13), D)
    sign_pattern = jnp.where(shuffled < D // 2, 1.0, -1.0).astype(jnp.float32)
    offsets = jax.random.randint(jax.random.fold_in(key, 17), (HEADS,), 0, HEAD_DIM)
    columns = jnp.arange(HEADS, dtype=jnp.int32) * HEAD_DIM + offsets
    picked = jnp.any(jnp.arange(D, dtype=jnp.int32)[:, None] == columns[None, :], axis=1).astype(jnp.float32)
    return (sign_pattern, picked)


def draw_global_pos(key, part):
    return global_positions(key)


def draw_tokens(key, part):
    sign_pattern, picked = shared_pattern(key)
    flagged = jax.random.randint(jax.random.fold_in(key, 31), (H * W,), 0, 20) == 0
    forced = jnp.zeros((H * W,), jnp.int32).at[global_positions(key)[:max(GLOBALS // 8, 1)]].set(1)
    outlier = (flagged | (forced > 0)).astype(jnp.float32)
    noise = jax.random.truncated_normal(jax.random.fold_in(key, 29), -6.0, 6.0, (H * W, D), jnp.float32)
    amplitude = jnp.exp(jax.random.uniform(jax.random.fold_in(key, 37), (H * W,), jnp.float32, math.log(0.5), math.log(2.5)))
    result = noise + (outlier * amplitude)[:, None] * sign_pattern[None, :]
    return result.reshape(H, W, D).astype(jnp.bfloat16)


def draw_w_query(key, part):
    sign_pattern, picked = shared_pattern(key)
    base = jax.random.truncated_normal(jax.random.fold_in(key, 21), -6.0, 6.0, (D, D), jnp.float32) * D ** (-0.5)
    boost = outlier_gain / D * sign_pattern[:, None] * picked[None, :]
    return (base + boost).astype(jnp.bfloat16)


def draw_w_keyval(key, part):
    sign_pattern, picked = shared_pattern(key)
    base = jax.random.truncated_normal(jax.random.fold_in(key, 23), -6.0, 6.0, (D, 2, D), jnp.float32) * D ** (-0.5)
    halves = jnp.array([1.0, 0.0], jnp.float32)
    boost = outlier_gain / D * sign_pattern[:, None, None] * halves[None, :, None] * picked[None, None, :]
    return (base + boost).astype(jnp.bfloat16)


def with_ends(values, rng, smallest, top_value):
    extent = values.shape
    place = [jax.random.randint(jax.random.fold_in(rng, axis), (), 0, extent[axis]) for axis in range(len(extent))]
    values = values.at[tuple(place)].set(smallest)
    longest = extent.index(max(extent))
    place[longest] = (place[longest] + 1) % extent[longest]
    return values.at[tuple(place)].set(top_value)


def steps_of(rng, shape, cuts, least, largest):
    gain, own = 1.0, jax.random.fold_in(rng, 6)
    for position, shards_of in cuts:
        steps = jnp.exp(jax.random.uniform(jax.random.fold_in(own, position), (shards_of,), jnp.float32, least / len(cuts), largest / len(cuts)))
        gain = gain * jnp.repeat(steps, shape[position] // shards_of).reshape([-1 if axis == position else 1 for axis in range(len(shape))])
    return gain


def bell_draw(rng, extent, deviation, bound, split=(), held_as=jnp.bfloat16):
    values = jax.random.normal(rng, extent, jnp.float32) * deviation
    if len(split) > 0:
        values = steps_of(rng, extent, split, -0.22, 0.18) * values
    return jnp.clip(values, min=-bound, max=bound).astype(held_as)


def setup_inputs(seed: int = 0) -> dict:
    arg_keys = jax.random.split(jax.random.key(seed), 7)
    return {
        "tokens": draw_tokens(jax.random.fold_in(arg_keys[6], 71), 0),
        "tissue": with_ends((jax.random.randint(arg_keys[1], (H, W), 0, 4) < 3).astype(jnp.int32), jax.random.fold_in(arg_keys[1], 1), 0, 1),
        "global_pos": draw_global_pos(jax.random.fold_in(arg_keys[6], 71), 0),
        "w_query": draw_w_query(jax.random.fold_in(arg_keys[6], 71), 0),
        "w_keyval": draw_w_keyval(jax.random.fold_in(arg_keys[6], 71), 0),
        "w_out": bell_draw(arg_keys[5], (D, D), D ** -0.5, 0.3125, ((0, 2),)),
    }


def layer_norm(tokens):
    values = tokens.astype(jnp.float32)
    center = values - lax.optimization_barrier(jnp.mean(values, axis=-1, keepdims=True))
    spread = lax.optimization_barrier(jnp.mean(center * center, axis=-1, keepdims=True))
    return (center * lax.rsqrt(spread + 1e-05)).astype(jnp.bfloat16)

def attend_block(query_blk, key_blk, value_blk, mask_blk, glob_key, glob_value):
    head_count = query_blk.shape[-2]
    head_depth = query_blk.shape[-1]
    span_rows = BR + 2 * WIN
    span_cols = BC + 2 * WIN
    query_flat = query_blk.reshape(BR * BC, head_count, head_depth).astype(jnp.float32)
    key_flat = key_blk.reshape(span_rows * span_cols, head_count, head_depth).astype(jnp.float32)
    value_flat = value_blk.reshape(span_rows * span_cols, head_count, head_depth).astype(jnp.float32)
    score_win = jnp.einsum('qhd,khd->hqk', query_flat, key_flat)
    score_glob = jnp.einsum('qhd,ghd->hqg', query_flat, glob_key.astype(jnp.float32))
    query_row = jnp.repeat(jnp.arange(BR), BC)
    query_col = jnp.tile(jnp.arange(BC), BR)
    key_row = jnp.repeat(jnp.arange(span_rows), span_cols)
    key_col = jnp.tile(jnp.arange(span_cols), span_rows)
    delta_row = key_row[None, :] - query_row[:, None]
    delta_col = key_col[None, :] - query_col[:, None]
    inside = (delta_row >= 0) & (delta_row <= 2 * WIN) & (delta_col >= 0) & (delta_col <= 2 * WIN)
    inside = inside & (mask_blk.reshape(-1)[None, :] > 0.5)
    score_win = jnp.where(inside[None], score_win, -1e+30)
    peak = jnp.maximum(lax.optimization_barrier(jnp.max(score_win, axis=-1)), lax.optimization_barrier(jnp.max(score_glob, axis=-1)))
    prob_win = jnp.exp(score_win - peak[..., None])
    prob_glob = jnp.exp(score_glob - peak[..., None])
    totals = lax.optimization_barrier(jnp.sum(prob_win, axis=-1)) + lax.optimization_barrier(jnp.sum(prob_glob, axis=-1))
    weight_win = (prob_win / totals[..., None]).astype(jnp.bfloat16).astype(jnp.float32)
    weight_glob = (prob_glob / totals[..., None]).astype(jnp.bfloat16).astype(jnp.float32)
    result = jnp.einsum('hqk,khd->qhd', weight_win, value_flat)
    return result + jnp.einsum('hqg,ghd->qhd', weight_glob, glob_value.astype(jnp.float32))

def window_part(query_grid, key_ext, value_ext, mask_ext, glob_key, glob_value):
    grid_rows, grid_cols, head_count, head_depth = query_grid.shape
    block_rows = grid_rows // BR
    block_cols = grid_cols // BC

    def one_row(row_index):
        row_start = (row_index * BR).astype(jnp.int32)
        query_rows = lax.dynamic_slice_in_dim(query_grid, row_start, BR, 0)
        key_rows = lax.dynamic_slice_in_dim(key_ext, row_start, BR + 2 * WIN, 0)
        value_rows = lax.dynamic_slice_in_dim(value_ext, row_start, BR + 2 * WIN, 0)
        mask_rows = lax.dynamic_slice_in_dim(mask_ext, row_start, BR + 2 * WIN, 0)

        def one_block(col_index):
            col_start = (col_index * BC).astype(jnp.int32)
            return attend_block(lax.dynamic_slice_in_dim(query_rows, col_start, BC, 1), lax.dynamic_slice_in_dim(key_rows, col_start, BC + 2 * WIN, 1), lax.dynamic_slice_in_dim(value_rows, col_start, BC + 2 * WIN, 1), lax.dynamic_slice_in_dim(mask_rows, col_start, BC + 2 * WIN, 1), glob_key, glob_value)
        return jax.vmap(one_block)(jnp.arange(block_cols, dtype=jnp.int32))
    stacked = lax.map(one_row, jnp.arange(block_rows, dtype=jnp.int32))
    stacked = stacked.reshape(block_rows, block_cols, BR, BC, head_count * head_depth)
    return stacked.transpose(0, 2, 1, 3, 4).reshape(grid_rows * grid_cols, head_count * head_depth)

def tile_partial(glob_query, key_tile, value_tile, mask_tile):
    score = jnp.einsum('ghd,nhd->hgn', glob_query.astype(jnp.float32), key_tile.astype(jnp.float32))
    valid = (mask_tile > 0.5)[None, None, :]
    score = jnp.where(valid, score, -1e+30)
    peak = lax.optimization_barrier(jnp.max(score, axis=-1))
    expo = jnp.where(valid, jnp.exp(score - peak[..., None]), 0.0)
    totals = lax.optimization_barrier(jnp.sum(expo, axis=-1))
    weight = expo.astype(jnp.bfloat16).astype(jnp.float32)
    numer = jnp.einsum('hgn,nhd->ghd', weight, value_tile.astype(jnp.float32))
    return (peak.T, totals.T, numer)

def combine(earlier, later):
    peak = jnp.maximum(earlier[0], later[0])
    factor_a = jnp.exp(earlier[0] - peak)
    factor_b = jnp.exp(later[0] - peak)
    return (peak, earlier[1] * factor_a + later[1] * factor_b, earlier[2] * factor_a[..., None] + later[2] * factor_b[..., None])

def reference(tokens, tissue, global_pos, w_query, w_keyval, w_out):
    query_scale = HEAD_DIM ** (-0.5)
    normed = layer_norm(tokens).reshape(H * W, D)
    query = (jnp.dot(normed, w_query, preferred_element_type=jnp.float32) * query_scale).astype(jnp.bfloat16)
    keys = jnp.dot(normed, w_keyval[:, 0, :], preferred_element_type=jnp.float32).astype(jnp.bfloat16)
    values = jnp.dot(normed, w_keyval[:, 1, :], preferred_element_type=jnp.float32).astype(jnp.bfloat16)
    maskf = tissue.astype(jnp.float32)
    glob_query = query[global_pos].reshape(GLOBALS, HEADS, HEAD_DIM)
    glob_keys = keys[global_pos].reshape(GLOBALS, HEADS, HEAD_DIM)
    glob_values = values[global_pos].reshape(GLOBALS, HEADS, HEAD_DIM)
    query_grid = query.reshape(H, W, HEADS, HEAD_DIM)
    key_grid = keys.reshape(H, W, HEADS, HEAD_DIM)
    value_grid = values.reshape(H, W, HEADS, HEAD_DIM)
    padding = ((WIN, WIN), (WIN, WIN), (0, 0), (0, 0))
    window_out = window_part(query_grid, jnp.pad(key_grid, padding), jnp.pad(value_grid, padding), jnp.pad(maskf, ((WIN, WIN), (WIN, WIN))), glob_keys, glob_values)

    def step(carry, tile_index):
        tile_row = (tile_index // N_COL).astype(jnp.int32)
        tile_col = (tile_index % N_COL).astype(jnp.int32)
        row_start = (tile_row * CH).astype(jnp.int32)
        col_start = (tile_col * CW).astype(jnp.int32)
        zero_index = jnp.zeros((), jnp.int32)
        key_tile = lax.dynamic_slice(key_grid, (row_start, col_start, zero_index, zero_index), (CH, CW, HEADS, HEAD_DIM))
        value_tile = lax.dynamic_slice(value_grid, (row_start, col_start, zero_index, zero_index), (CH, CW, HEADS, HEAD_DIM))
        mask_tile = lax.dynamic_slice(maskf, (row_start, col_start), (CH, CW))
        part = tile_partial(glob_query, key_tile.reshape(CH * CW, HEADS, HEAD_DIM), value_tile.reshape(CH * CW, HEADS, HEAD_DIM), mask_tile.reshape(-1))
        return (combine(carry, part), None)
    start = tile_partial(glob_query, glob_keys, glob_values, jnp.ones((GLOBALS,), jnp.float32))
    final, _ = lax.scan(step, start, jnp.arange(N_ROW * N_COL, dtype=jnp.int32))
    glob_out = (final[2] / final[1][..., None]).reshape(GLOBALS, D)
    attn = window_out.at[global_pos].set(glob_out).astype(jnp.bfloat16)
    mixed = jnp.dot(attn, w_out, preferred_element_type=jnp.float32).astype(jnp.bfloat16)
    return mixed.reshape(H, W, D)
```

```python
import functools

import jax
import jax.numpy as jnp
from jax import lax
from jax.experimental import pallas as pl
from jax.experimental.pallas import tpu as pltpu
from jax.sharding import PartitionSpec as P

HEAD_DIM = 64
WIN = 7
BR = 8
BC = 16
GRP = 128
EDGE = 8
SENTINEL = 100.0
BIG = -1e30
ROW0, LOW0, HIGH0, TIS = 64, 80, 96, 112
AXES = ("row", "col", "head")
F32 = jnp.float32
BF16 = jnp.bfloat16


def iota(shape, dim):
    return lax.broadcasted_iota(jnp.int32, shape, dim)


def dot(a, b, ca=1, cb=0):
    return lax.dot_general(a, b, (((ca,), (cb,)), ((), ())), preferred_element_type=F32)


def normalize(values):
    center = values - jnp.mean(values, axis=-1, keepdims=True)
    spread = jnp.mean(center * center, axis=-1, keepdims=True)
    return center * lax.rsqrt(spread + 1e-05)


def whole(shape):
    return pl.BlockSpec(memory_space=pltpu.VMEM)


def call(kernel, outs, *args, scratch=(), flops=10**9, name=None):
    return pl.pallas_call(
        kernel,
        out_shape=outs,
        in_specs=[pl.BlockSpec(memory_space=pltpu.VMEM)] * len(args),
        out_specs=jax.tree.map(lambda _: pl.BlockSpec(memory_space=pltpu.VMEM), outs),
        scratch_shapes=list(scratch),
        compiler_params=pltpu.CompilerParams(vmem_limit_bytes=56 * 2**20),
        cost_estimate=pl.CostEstimate(flops=flops, bytes_accessed=2**20, transcendentals=0),
        name=name,
    )(*args)


def tissue_feature(excluded, shape):
    return jnp.where((iota(shape, 1) % GRP == TIS) & excluded, BIG, 0.0)


def local_kernel(tok_ref, mark_ref, wq_ref, wk_ref, wv_ref, q_ref, k_ref, vt_ref):
    normed = normalize(tok_ref[...].astype(F32)).astype(BF16)
    q_ref[...] = (dot(normed, wq_ref[...]) * HEAD_DIM**-0.5).astype(BF16)
    excluded = mark_ref[:, :1].astype(F32) > SENTINEL / 2
    keys = dot(normed, wk_ref[...])
    k_ref[...] = (keys + tissue_feature(excluded, keys.shape)).astype(BF16)
    vt_ref[...] = dot(wv_ref[...], normed, 0, 1).astype(BF16)


def extended_kernel(tok_ref, top_ref, bot_ref, left_ref, right_ref, wk_ref, wv_ref, k_ref, vt_ref, ext_ref):
    rows, cols = tok_ref.shape[0], tok_ref.shape[1]
    halves, ext_rows = ext_ref.shape[0], ext_ref.shape[1]

    def put(values, row, col8):
        count = values.shape[0]
        ext_ref[col8 // 2, row : row + count, (col8 % 2) * 8 : (col8 % 2) * 8 + 8, :] = values

    def strip(ref, lo):
        return ref[:, lo : lo + 8, :].astype(F32)

    for piece in range(cols // 8):
        put(strip(tok_ref, piece * 8), WIN, piece + 1)
        put(strip(top_ref, piece * 8), 0, piece + 1)
        put(strip(bot_ref, piece * 8), WIN + rows, piece + 1)
    put(strip(left_ref, 0), 0, 0)
    put(strip(right_ref, 0), 0, cols // 8 + 1)
    used = rows + 2 * WIN
    ext_ref[:, used:, :, :] = jnp.full((halves, ext_rows - used, BC, ext_ref.shape[3]), SENTINEL, F32)
    per = ext_rows * BC
    for half in range(halves):
        values = ext_ref[half].reshape(per, ext_ref.shape[3])
        excluded = values[:, :1] > SENTINEL / 2
        normed = normalize(values).astype(BF16)
        keys = dot(normed, wk_ref[...])
        lane = iota((per, GRP), 1)
        place = iota((per, GRP), 0)
        key_row, key_col = place // BC, place % BC
        query_row, low, high = lane - ROW0, lane - LOW0, lane - HIGH0
        out_row = (query_row >= 0) & (query_row < rows)
        out_row = out_row & ((key_row < query_row) | (key_row > query_row + 2 * WIN))
        out_low = (low >= 0) & (low < BC) & (key_col <= low)
        out_high = (high >= 0) & (high < BC) & (key_col >= high)
        bias = jnp.where(out_row | out_low | out_high, BIG, 0.0)
        bias = jnp.where((lane == TIS) & excluded, BIG, bias)
        for head in range(keys.shape[1] // GRP):
            lanes = slice(head * GRP, (head + 1) * GRP)
            k_ref[half * per : (half + 1) * per, lanes] = (keys[:, lanes] + bias).astype(BF16)
        vt_ref[:, half * per : (half + 1) * per] = dot(wv_ref[...], normed, 0, 1).astype(BF16)


def softmax_part(key, query, value_t):
    score = dot(key, query, 1, 1)
    peak = jnp.max(score, axis=0, keepdims=True)
    expo = jnp.exp(score - peak)
    return peak, jnp.sum(expo, axis=0, keepdims=True), dot(value_t, expo.astype(BF16))


def store_part(ref, head, heads, part):
    peak, total, numer = part
    base = heads * HEAD_DIM
    ref[head * HEAD_DIM : (head + 1) * HEAD_DIM, :] = numer
    ref[base + head : base + head + 1, :] = peak
    ref[base + heads + head : base + heads + head + 1, :] = total


def global_kernel(tok_ref, wq_ref, wk_ref, wv_ref, k_ref, vt_ref, kg_ref, vgt_ref, part_ref, own_ref):
    normed = normalize(tok_ref[...].astype(F32)).astype(BF16)
    query = dot(normed, wq_ref[...]) * HEAD_DIM**-0.5
    query = (query + jnp.where(iota(query.shape, 1) % GRP == TIS, 1.0, 0.0)).astype(BF16)
    keys = dot(normed, wk_ref[...]).astype(BF16)
    values_t = dot(wv_ref[...], normed, 0, 1).astype(BF16)
    kg_ref[...] = keys
    vgt_ref[...] = values_t
    heads = keys.shape[1] // GRP
    pad = part_ref.shape[0] - heads * (HEAD_DIM + 2)
    for head in range(heads):
        lanes = slice(head * GRP, (head + 1) * GRP)
        rows = slice(head * HEAD_DIM, (head + 1) * HEAD_DIM)
        part = softmax_part(k_ref[:, lanes], query[:, lanes], vt_ref[rows, :])
        store_part(part_ref, head, heads, part)
        store_part(own_ref, head, heads, softmax_part(keys[:, lanes], query[:, lanes], values_t[rows, :]))
    part_ref[part_ref.shape[0] - pad :, :] = jnp.zeros((pad, part_ref.shape[1]), F32)
    own_ref[part_ref.shape[0] - pad :, :] = jnp.zeros((pad, part_ref.shape[1]), F32)


def merge_kernel(heads, final, *refs):
    ins, out_ref = refs[:-1], refs[-1]
    base = heads * HEAD_DIM
    if not final:
        out_ref[...] = jnp.zeros(out_ref.shape, F32)
    for head in range(heads):
        rows = slice(head * HEAD_DIM, (head + 1) * HEAD_DIM)
        peaks = [ref[base + head : base + head + 1, :] for ref in ins]
        peak = functools.reduce(jnp.maximum, peaks)
        numer, total = 0.0, 0.0
        for ref, own in zip(ins, peaks):
            factor = jnp.exp(own - peak)
            numer = numer + ref[rows, :] * factor
            total = total + ref[base + heads + head : base + heads + head + 1, :] * factor
        if final:
            out_ref[rows, :] = (numer / total).astype(BF16)
        else:
            out_ref[rows, :] = numer
            out_ref[base + head : base + head + 1, :] = peak
            out_ref[base + heads + head : base + heads + head + 1, :] = total


def window_kernel(br, q_ref, k_ref, vt_ref, kg_ref, vgt_ref, out_ref):
    cols = q_ref.shape[1]
    heads = q_ref.shape[2] // GRP
    per = k_ref.shape[0] // (cols // BC + 1)
    count = (BR + 2 * WIN) * BC
    cells = BR * BC
    place, lane = iota((cells, GRP), 0), iota((cells, GRP), 1)
    row_hot = lane - ROW0 == place // BC + br * BR
    low_hot = lane - LOW0 == place % BC
    high_hot = lane - HIGH0 == place % BC
    tissue_hot = lane == TIS
    aug_low = jnp.where(row_hot | low_hot | tissue_hot, 1.0, 0.0).astype(BF16)
    aug_high = jnp.where(row_hot | high_hot | tissue_hot, 1.0, 0.0).astype(BF16)
    for bc in range(cols // BC):
        first = bc * per + br * BR * BC
        second = first + per
        pieces = []
        for head in range(heads):
            lanes = slice(head * GRP, (head + 1) * GRP)
            rows = slice(head * HEAD_DIM, (head + 1) * HEAD_DIM)
            query = q_ref[:, bc * BC : (bc + 1) * BC, lanes].reshape(cells, GRP)
            score = [
                dot(k_ref[first : first + count, lanes], query + aug_low, 1, 1),
                dot(k_ref[second : second + count, lanes], query + aug_high, 1, 1),
                dot(kg_ref[:, lanes], query, 1, 1),
            ]
            peak = functools.reduce(jnp.maximum, [jnp.max(s, axis=0, keepdims=True) for s in score])
            expo = [jnp.exp(s - peak) for s in score]
            total = sum(jnp.sum(e, axis=0, keepdims=True) for e in expo)
            scale = 1.0 / total
            prob = [(e * scale).astype(BF16) for e in expo]
            value = [
                vt_ref[rows, first : first + count],
                vt_ref[rows, second : second + count],
                vgt_ref[rows, :],
            ]
            pieces.append(sum(dot(v, p) for v, p in zip(value, prob)))
        block = jnp.concatenate(pieces, axis=0).T.astype(BF16)
        out_ref[:, bc * BC : (bc + 1) * BC, :] = block.reshape(BR, BC, heads * HEAD_DIM)


def final_kernel(slot_ref, own_ref, other_ref, gown_ref, gother_ref, wown_ref, wother_ref, out_ref):
    rows = own_ref.shape[0]
    mixed = dot(own_ref[...], wown_ref[...]) + dot(other_ref[...], wother_ref[...])
    special = dot(gown_ref[...], wown_ref[...], 0, 0) + dot(gother_ref[...], wother_ref[...], 0, 0)
    hot = jnp.where(iota((rows, slot_ref.shape[1]), 0) == slot_ref[...], 1.0, 0.0)
    picked = dot(hot.astype(BF16), special.astype(BF16))
    is_special = jnp.sum(hot, axis=1, keepdims=True) > 0.5
    out_ref[...] = jnp.where(is_special, picked, mixed).astype(BF16)


def device_perm(sizes, move):
    rows, cols, heads = sizes
    pairs = []
    for r in range(rows):
        for c in range(cols):
            for h in range(heads):
                target = move(r, c, h)
                if target is None:
                    continue
                tr, tc, th = target
                if 0 <= tr < rows and 0 <= tc < cols:
                    pairs.append(((r * cols + c) * heads + h, (tr * cols + tc) * heads + th))
    return pairs


def partner(index, step, size):
    return index ^ step if size & (size - 1) == 0 else (index + step) % size


def gathered(value, sizes, stage):
    rows, cols, _ = sizes
    swap = rows == cols
    outs = []
    for step in range(1, rows if stage == 0 or swap else cols):

        def move(r, c, h, step=step):
            along_row = (stage == 0) != (swap and h == 1)
            return (partner(r, step, rows), c, h) if along_row else (r, partner(c, step, cols), h)

        outs.append(lax.ppermute(value, AXES, device_perm(sizes, move)))
    return outs


def swapped(value):
    return lax.ppermute(value, "head", [(0, 1), (1, 0)])


def on_device(tokens, tissue, global_pos, w_query, w_keyval, w_out):
    tile_rows, tile_cols, width = tokens.shape
    cells = tile_rows * tile_cols
    sizes = tuple(lax.axis_size(axis) for axis in AXES)
    row, col, core = (lax.axis_index(axis) for axis in AXES)
    heads = w_query.shape[1] // HEAD_DIM
    group = heads * HEAD_DIM
    glob_count = global_pos.shape[0]
    half_count = glob_count // 2
    flat = tokens.reshape(cells, width)
    marked = jnp.where(tissue[..., None] == 1, tokens, jnp.asarray(SENTINEL, BF16))

    image_cols = tile_cols * sizes[1]
    glob_row, glob_col = global_pos // image_cols - row * tile_rows, global_pos % image_cols - col * tile_cols
    here = (glob_row >= 0) & (glob_row < tile_rows) & (glob_col >= 0) & (glob_col < tile_cols)
    slot = jnp.where(here, glob_row * tile_cols + glob_col, cells)
    half_slot = lax.dynamic_slice_in_dim(slot, core * half_count, half_count)
    hot = (half_slot[:, None] == jnp.arange(cells, dtype=jnp.int32)[None, :]).astype(BF16)
    glob = jnp.dot(hot, flat, preferred_element_type=F32).astype(BF16)
    for stage in range(2):
        glob = sum(gathered(glob, sizes, stage), glob)
    glob_other = swapped(glob)
    glob_tokens = jnp.where(core == 0, jnp.stack([glob, glob_other]), jnp.stack([glob_other, glob]))
    glob_tokens = glob_tokens.reshape(glob_count, width)

    first_core = core == 0
    row_move = lambda r, c, h: (r - 1 if h == 0 else r + 1, c, h)
    col_move = lambda r, c, h: (r, c - 1 if h == 0 else c + 1, h)
    edge = jnp.where(first_core, marked[:WIN], marked[-WIN:])
    got = lax.ppermute(edge, AXES, device_perm(sizes, row_move))
    outside = jnp.where(first_core, row == sizes[0] - 1, row == 0)
    got = jnp.where(outside, jnp.asarray(SENTINEL, BF16), got)
    got_other = swapped(got)
    top = jnp.where(first_core, got_other, got)
    bottom = jnp.where(first_core, got, got_other)
    side = lambda part: jnp.where(first_core, part[:, :EDGE], part[:, -EDGE:])
    edge = jnp.concatenate([side(top), side(marked), side(bottom)], axis=0)
    got = lax.ppermute(edge, AXES, device_perm(sizes, col_move))
    outside = jnp.where(first_core, col == sizes[1] - 1, col == 0)
    got = jnp.where(outside, jnp.asarray(SENTINEL, BF16), got)
    got_other = swapped(got)
    left = jnp.where(first_core, got_other, got)
    right = jnp.where(first_core, got, got_other)

    pad_heads = lambda w: jnp.pad(
        w.reshape(width, heads, HEAD_DIM), ((0, 0), (0, 0), (0, GRP - HEAD_DIM))
    ).reshape(width, heads * GRP)
    w_q, w_k, w_v = pad_heads(w_query), pad_heads(w_keyval[:, 0]), w_keyval[:, 1]
    out_cols = w_out.shape[1] // 2
    w_cols = [w_out[:, :out_cols], w_out[:, out_cols:]]
    w_own = jnp.where(first_core, w_cols[0], w_cols[1])
    w_other = swapped(jnp.where(first_core, w_cols[1], w_cols[0]))

    sds = jax.ShapeDtypeStruct
    wide = heads * GRP
    query, key_loc, value_loc = call(
        local_kernel,
        (sds((cells, wide), BF16), sds((cells, wide), BF16), sds((group, cells), BF16)),
        flat, marked.reshape(cells, width), w_q, w_k, w_v,
        name="local",
    )
    halves, ext_rows = tile_cols // BC + 1, tile_rows + 2 * BR
    ext_cells = halves * ext_rows * BC
    key_ext, value_ext = call(
        extended_kernel,
        (sds((ext_cells, wide), BF16), sds((group, ext_cells), BF16)),
        marked, top, bottom, left, right, w_k, w_v,
        scratch=[pltpu.VMEM((halves, ext_rows, BC, width), F32)],
        name="extended",
    )
    part_rows = -(-heads * (HEAD_DIM + 2) // 8) * 8
    part = sds((part_rows, glob_count), F32)
    key_glob, value_glob, local_part, glob_part = call(
        global_kernel,
        (sds((glob_count, wide), BF16), sds((group, glob_count), BF16), part, part),
        glob_tokens, w_q, w_k, w_v, key_loc, value_loc,
        name="globals",
    )
    query_grid = query.reshape(tile_rows, tile_cols, wide)
    window = []
    for br in range(tile_rows // BR):
        window.append(
            call(
                functools.partial(window_kernel, br),
                sds((BR, tile_cols, group), BF16),
                query_grid[br * BR : (br + 1) * BR], key_ext, value_ext, key_glob, value_glob,
                name=f"window{br}",
            )
        )
    merged = local_part
    for stage in range(2):
        pieces = [merged] + gathered(merged, sizes, stage)
        if stage == 0:
            merged = call(functools.partial(merge_kernel, heads, False), part, *pieces, name="merge0")
        else:
            glob_out = call(
                functools.partial(merge_kernel, heads, True), sds((group, glob_count), BF16),
                *pieces, glob_part, name="merge1",
            )
    glob_out_other = swapped(glob_out)
    attn = jnp.concatenate(window, axis=0).reshape(cells, group)
    attn_other = swapped(attn)
    mixed = call(
        final_kernel,
        sds((cells, out_cols), BF16),
        slot.reshape(1, glob_count), attn, attn_other, glob_out, glob_out_other, w_own, w_other,
        name="final",
    )
    return mixed.reshape(tile_rows, tile_cols, out_cols)


def solution(mesh):
    in_specs = (
        P("row", "col", None),
        P("row", "col"),
        P(),
        P(None, "head"),
        P(None, None, "head"),
        P("head", None),
    )
    return jax.shard_map(
        on_device, mesh=mesh, in_specs=in_specs, out_specs=P("row", "col", "head"), check_vma=False
    )
```
